32 devices in a mesh: rows: 8 (over y, x, core), probe: 4 (over z).
Axes of the slice: x: 2, y: 2, z: 4, core: 2. Of those that a mesh axis runs over, the one named last changes fastest.
Arguments:
- points: float32 [64, 3, 128], P('rows'), may hold values from 0 to 1
- observations: float32 [64, 128], P('rows'), may hold values from -6 to 6
- probes: float32 [64, 64, 128], P('rows', 'probe'), may hold values from -150 to 150
- neighbours: int32 [64, 3], P('rows'), may hold values from 0 to 63, as said below
- block_position: int32 [64], P('rows'), may hold values from 0 to 63, as said below
Outputs:
- whitened: float32 [64, 128], P('rows')
- block_terms: float32 [64], P('rows')
- tridiagonal: float32 [64, 3], P('probe')
- remainder: float32 [64, 64, 128], P('rows', 'probe')
The draws below stay inside these ranges and needn't reach their ends.
Inputs may be any that keep to these rules, and one draw needn't show every extreme that they name: block_position is a permutation of the block ids; the block with id i sits at position block_position[i], on index block_position[i] // 8 of rows. neighbours[b] lists three block ids, which may repeat and may name the block at b itself. Over the 24 references of the blocks of one index of rows, the positions of the named blocks fall at most 6 times on the blocks of any one index of rows, and exactly 6 times on those of some index, for every index.
All inputs are finite; a program needn't handle non-finite values.
Results may differ from the reference program's by a relative error of at most 0.0003.
Values sent between devices are 32-bit elements; how exact they have to be, the bound alone decides.
A program may use at most 64 MiB of HBM per device.

```python
import math
import jax
import jax.numpy as jnp
from jax import lax

BS = 128
BLK_DEV = 8
PROBES = 64
NB = 64
CAP = 6


def neighbour_layout(key):
    base_key = jax.random.fold_in(key, 7)
    devices = NB // BLK_DEV
    references = 3 * BLK_DEV
    slot_count = devices * CAP

    def per_device(device):
        dev_key = jax.random.fold_in(base_key, device)
        key_one, key_two, key_three, key_four = jax.random.split(dev_key, 4)
        forced = jax.random.randint(key_one, (), 0, devices)
        slot_ids = jnp.arange(slot_count, dtype=jnp.int32)
        slot_owner = slot_ids // CAP
        distance = jnp.abs(slot_owner - device)
        jitter = jax.random.randint(key_two, (slot_count,), 0, 1024)
        scores = jitter * 4096 + slot_ids - distance * (1 << 20) + jnp.where(slot_owner == forced, 1 << 28, 0)
        top_scores, chosen = lax.top_k(scores, references)
        shuffle = jax.random.permutation(key_three, references)
        owners = (chosen // CAP)[shuffle]
        local_rows = jax.random.randint(key_four, (references,), 0, BLK_DEV)
        return owners * BLK_DEV + local_rows
    positions = jax.vmap(per_device)(jnp.arange(devices, dtype=jnp.int32))
    placement_perm = jax.random.permutation(jax.random.fold_in(base_key, 100003), NB).astype(jnp.int32)
    id_at = jnp.argsort(placement_perm).astype(jnp.int32)
    near_ids = id_at[positions.reshape(NB, 3)]
    return (near_ids.astype(jnp.int32), placement_perm)


def draw_neighbours(key, part):
    return neighbour_layout(key)[0]


def draw_block_position(key, part):
    return neighbour_layout(key)[1]


def draw_probes(key, part):
    key_one, key_two, key_three = jax.random.split(jax.random.fold_in(key, 11), 3)
    position_trend = jnp.arange(NB, dtype=jnp.float32) / NB
    roughness = jax.random.uniform(key_two, (NB,), jnp.float32, -0.7, 0.7)
    column = jax.random.uniform(key_three, (PROBES,), jnp.float32, -1.1, 1.1)
    base_draw = jnp.clip(jax.random.normal(key_one, (NB, PROBES, BS), jnp.float32), -4.0, 4.0)
    growth = 1.1
    scaling = jnp.exp(growth * position_trend + roughness)[:, None, None] * jnp.exp(column)[None, :, None]
    return base_draw * scaling


def block_levels(own_key, extent, cuts, least, top_value):
    factor_of, own = 1.0, jax.random.fold_in(own_key, 6)
    for dim, blocks in cuts:
        steps = jnp.exp(jax.random.uniform(jax.random.fold_in(own, dim), (blocks,), jnp.float32, least / len(cuts), top_value / len(cuts)))
        factor_of = factor_of * jnp.repeat(steps, extent[dim] // blocks).reshape([-1 if axis == dim else 1 for axis in range(len(extent))])
    return factor_of


def gaussian(key, dims, scale, most, shards=(), kind=jnp.bfloat16):
    result = scale * jax.random.normal(key, dims, jnp.float32)
    if shards:
        result = result * block_levels(key, dims, shards, -0.22, 0.18)
    return jnp.clip(result, -most, most).astype(kind)


def setup_inputs(seed: int = 0) -> dict:
    key_list = jax.random.split(jax.random.key(seed), 6)
    points = jnp.clip(1.0 * jax.random.uniform(key_list[0], (NB, 3, BS), jnp.float32) ** block_levels(key_list[0], (NB, 3, BS), ((0, 8),), -0.2, 0.2), 0.0, 1.0)
    observations = gaussian(key_list[1], (NB, BS), 1.0, 6.0, ((0, 8),), jnp.float32)
    probes = draw_probes(jax.random.fold_in(key_list[5], 71), 0)
    neighbours = draw_neighbours(jax.random.fold_in(key_list[5], 71), 0)
    block_position = draw_block_position(jax.random.fold_in(key_list[5], 71), 0)
    return {"points": points, "observations": observations, "probes": probes, "neighbours": neighbours, "block_position": block_position}


length_scale = 0.3
nugget = 0.25
epsilon = 1e-06
highest = lax.Precision.HIGHEST

def factor_block(inputs):
    near_points, own_points, near_values, own_values = inputs
    block_size = own_points.shape[-1]
    point_set = jnp.concatenate([jnp.transpose(near_points, (1, 0, 2)).reshape(3, 3 * block_size), own_points], axis=1)
    offsets = point_set[:, :, None] - point_set[:, None, :]
    dist_sq = lax.optimization_barrier(jnp.sum(offsets * offsets, axis=0))
    matrix_order = 4 * block_size
    identity = jnp.eye(matrix_order, dtype=jnp.float32)
    kernel = 1.0 / (1.0 + dist_sq / (length_scale * length_scale)) + nugget * identity
    factor_low = jnp.linalg.cholesky(kernel)
    inverse = jax.scipy.linalg.solve_triangular(factor_low, identity, lower=True)
    conditioner = inverse[3 * block_size:]
    values = jnp.concatenate([near_values.reshape(3 * block_size), own_values])
    whitened = jnp.dot(conditioner, values, precision=highest)
    log_diag = jnp.sum(jnp.log(jnp.diagonal(factor_low)[3 * block_size:]))
    log_term = (-0.5 * jnp.sum(whitened * whitened) - log_diag) / block_size - 0.5 * math.log(2.0 * math.pi)
    return (conditioner, whitened, log_term)

def reference(points, observations, probes, neighbours, block_position):
    near_rows = block_position[neighbours]
    conditioner, whitened, block_terms = lax.map(factor_block, (points[near_rows], points, observations[near_rows], observations))
    cond_four = conditioner.reshape(NB, BS, 4, BS)
    flat_rows = near_rows.reshape(NB * 3)
    cells = NB * BS

    def apply_operator(vector):
        stacked = jnp.concatenate([vector[near_rows], vector[:, None]], axis=1)
        projected = jnp.einsum('bjpm,bkjm->bpk', stacked, cond_four, precision=highest)
        spread = jnp.einsum('bpk,bkjm->bjpm', projected, cond_four, precision=highest)
        moved = jnp.zeros_like(vector).at[flat_rows].add(spread[:, :3].reshape(NB * 3, PROBES, BS))
        return spread[:, 3] + moved

    def mean_inner(left, right):
        return lax.optimization_barrier(jnp.sum(left * right, axis=(0, 2))) / cells
    basis_one = probes / jnp.sqrt(mean_inner(probes, probes) + epsilon)[None, :, None]
    image_one = apply_operator(basis_one)
    alpha_one = mean_inner(basis_one, image_one)
    residue = image_one - alpha_one[None, :, None] * basis_one
    beta_one = jnp.sqrt(mean_inner(residue, residue) + epsilon)
    basis_two = residue / beta_one[None, :, None]
    image_two = apply_operator(basis_two)
    alpha_two = mean_inner(basis_two, image_two)
    remainder = image_two - alpha_two[None, :, None] * basis_two - beta_one[None, :, None] * basis_one
    tridiagonal = jnp.stack([alpha_one, beta_one, alpha_two], axis=1)
    return (whitened, block_terms, tridiagonal, remainder)
```

```python
import functools
import math

import jax
import jax.numpy as jnp
from jax import lax
from jax.experimental import pallas as pl
from jax.experimental.pallas import tpu as pltpu
from jax.sharding import PartitionSpec as P

length_scale = 0.3
nugget = 0.25
epsilon = 1e-06
highest = lax.Precision.HIGHEST
chunk = 8


def dot(left, right):
    return jnp.dot(left, right, precision=highest, preferred_element_type=jnp.float32)


def dot_nt(left, right):
    return lax.dot_general(
        left, right, (((1,), (1,)), ((), ())), precision=highest,
        preferred_element_type=jnp.float32,
    )


def invert_pivots(cols, units):
    cols = list(cols)
    width = len(cols)
    low = list(units)
    diag = None
    for k in range(width):
        at = units[k] > 0.5
        for i in range(k):
            low[i] = jnp.where(at, cols[i], low[i])
        diag = cols[k] if diag is None else jnp.where(at, cols[k], diag)
        pivot = jnp.broadcast_to(cols[k][k : k + 1, :], cols[k].shape)
        scaled = (cols[k] - units[k]) * (1.0 / pivot)
        for j in range(width):
            if j != k:
                cols[j] = cols[j] - scaled * jnp.broadcast_to(cols[j][k : k + 1, :], cols[j].shape)
        cols[k] = units[k] - scaled
    return cols, low, diag


def weighted(parts, rows):
    terms = [p * r for p, r in zip(parts, rows)]
    while len(terms) > 1:
        terms = [a + b for a, b in zip(terms[::2], terms[1::2])] + terms[len(terms) & ~1 :]
    return terms[0]


def sweep(mats):
    count = len(mats[0])
    shape = mats[0][0].shape
    lane = lax.broadcasted_iota(jnp.int32, shape, 1)
    sub = lax.broadcasted_iota(jnp.int32, shape, 0)
    units = [jnp.where(sub == k, 1.0, 0.0) for k in range(chunk)]

    def full(x):
        return jnp.broadcast_to(x, shape)

    mats = [list(m) for m in mats]
    logs = [jnp.zeros(shape, jnp.float32) for _ in mats]
    for t in range(count):
        o = t * chunk
        picked = (lane >= o) & (lane < o + chunk)
        unit = jnp.where(lane == sub + o, 1.0, 0.0)
        for b, chunks in enumerate(mats):
            top = chunks[t]
            inv, low, diag = invert_pivots([full(top[:, o + k : o + k + 1]) for k in range(chunk)], units)
            rows = jnp.where(picked, unit, top)
            rows = [full(rows[k : k + 1, :]) for k in range(chunk)]
            r = weighted(inv, rows)
            chunks[t] = lax.rsqrt(diag) * weighted(low, rows)
            logs[b] = logs[b] + jnp.log(diag)
            r = [full(r[k : k + 1, :]) for k in range(chunk)]
            for p in range(t + 1, count):
                old = chunks[p]
                cols = [full(old[:, o + k : o + k + 1]) for k in range(chunk)]
                chunks[p] = jnp.where(picked, 0.0, old) - weighted(cols, r)
    return mats, [-0.5 * jnp.sum(x[:, :1], axis=0, keepdims=True) for x in logs]


MESH = pl.DeviceIdType.MESH


def to_peers(axis, count, source, target, send_sem, recv_sem):
    me = lax.axis_index(axis)
    copies = []
    for p in range(1, count):
        peer = lax.rem(me + p, count)
        copies.append(
            pltpu.make_async_remote_copy(
                src_ref=source(peer),
                dst_ref=target,
                send_sem=send_sem.at[p - 1],
                recv_sem=recv_sem.at[p - 1],
                device_id={axis: peer},
                device_id_type=MESH,
            )
        )
    for copy in copies:
        copy.start()
    return copies


def wait_all(copies):
    for copy in copies:
        copy.wait()


def greet(counts):
    barrier = pltpu.get_barrier_semaphore()
    total = 0
    for axis, count in counts:
        for p in range(1, count):
            peer = lax.rem(lax.axis_index(axis) + p, count)
            pl.semaphore_signal(barrier, inc=1, device_id={axis: peer}, device_id_type=MESH)
            total += 1
    pl.semaphore_wait(barrier, total)


def gather_kernel(count, *refs):
    half = 4
    sources, targets, (send_sem, recv_sem, own_sem) = refs[:half], refs[half : 2 * half], refs[2 * half :]
    me = lax.axis_index("rows")
    greet((("rows", count),))
    copies = []
    for i in range(half):
        copies += to_peers(
            "rows", count, lambda peer: sources[i], targets[i].at[me], send_sem.at[i], recv_sem.at[i]
        )
    owns = [
        pltpu.make_async_copy(sources[i], targets[i].at[me], own_sem.at[i]) for i in range(half)
    ]
    for own in owns:
        own.start()
    for own in owns:
        own.wait()
    wait_all(copies)


def gather_rows(count, arrays):
    vmem = pl.BlockSpec(memory_space=pltpu.VMEM)
    return pl.pallas_call(
        functools.partial(gather_kernel, count),
        out_shape=[jax.ShapeDtypeStruct((count,) + a.shape, a.dtype) for a in arrays],
        in_specs=[vmem] * len(arrays),
        out_specs=[vmem] * len(arrays),
        scratch_shapes=[
            pltpu.SemaphoreType.DMA((len(arrays), count - 1)),
            pltpu.SemaphoreType.DMA((len(arrays), count - 1)),
            pltpu.SemaphoreType.DMA((len(arrays),)),
        ],
        compiler_params=pltpu.CompilerParams(collective_id=0, has_side_effects=True),
    )(*arrays)


def plan_kernel(capacity, first_ref, near_ref, pos_ref, slot_ref, local_ref, seen_ref):
    count, blocks = near_ref.shape[:2]
    me = first_ref[0]

    def position(owner, b, j):
        ident = near_ref[owner, b, j]
        return pos_ref[ident // blocks, 0, ident % blocks]

    for i in range(count * capacity):
        slot_ref[i] = 3 * blocks
        local_ref[i] = -1
    for i in range(count):
        seen_ref[i] = 0

    def place_own(b, c):
        for j in range(3):
            row = position(me, b, j)
            at = row // blocks
            rank = seen_ref[at]
            seen_ref[at] = rank + 1
            slot_ref[at * capacity + rank] = b * 3 + j
            local_ref[at * capacity + rank] = row % blocks
        return c

    lax.fori_loop(0, blocks, place_own, 0)


def plan_slots(first, near, positions, capacity):
    count = near.shape[0]
    smem = pl.BlockSpec(memory_space=pltpu.SMEM)
    slots = jax.ShapeDtypeStruct((count * capacity,), jnp.int32)
    return pl.pallas_call(
        functools.partial(plan_kernel, capacity),
        out_shape=(slots, slots),
        in_specs=[smem] * 3,
        out_specs=(smem, smem),
        scratch_shapes=[pltpu.SMEM((count,), jnp.int32)],
    )(first, near, positions)


def build_kernels(near_rows, me, first, points_ref, a_ref):
    nb = a_ref.shape[0]
    blocks, _, bs = points_ref.shape[1:]

    def part(i):
        return slice(i * bs, (i + 1) * bs)

    same = lax.broadcasted_iota(jnp.int32, (bs, bs), 0) == lax.broadcasted_iota(
        jnp.int32, (bs, bs), 1
    )
    for b in range(nb):
        at = [(row // blocks, row % blocks) for row in near_rows[b]] + [(me, first + b)]
        rows = [points_ref[o, r] for o, r in at]
        pad = jnp.zeros((chunk - rows[0].shape[0], bs), jnp.float32)
        cols = [jnp.transpose(jnp.concatenate([row, pad], axis=0)) for row in rows]
        for i in range(4):
            for k in range(i + 1):
                dist_sq = None
                for c in range(3):
                    off = cols[i][:, c : c + 1] - rows[k][c : c + 1, :]
                    dist_sq = off * off if dist_sq is None else dist_sq + off * off
                value = 1.0 / (1.0 + dist_sq * (1.0 / (length_scale * length_scale)))
                if i == k:
                    value = value + jnp.where(same, nugget, 0.0)
                a_ref[b, part(i), part(k)] = value


def factor_blocks(near_rows, me, first, values_ref, a_ref, g_ref, wt_ref):
    nb, bs = g_ref.shape[:2]
    blocks = values_ref.shape[1]

    def part(i):
        return slice(i * bs, (i + 1) * bs)

    def load(j):
        return tuple(
            tuple(
                a_ref[b, j * bs + i * chunk : j * bs + (i + 1) * chunk, part(j)]
                for i in range(bs // chunk)
            )
            for b in range(nb)
        )

    below = lax.broadcasted_iota(jnp.int32, (bs, bs), 0) >= lax.broadcasted_iota(
        jnp.int32, (bs, bs), 1
    )
    invs = []
    for j in range(4):
        low, logs = sweep(load(j))
        invs.append([jnp.where(below, jnp.concatenate(low[b], axis=0), 0.0) for b in range(nb)])
        if j == 3:
            break
        for b in range(nb):
            scaled = dot_nt(a_ref[b, (j + 1) * bs :, part(j)], invs[j][b])
            for i in range(j + 1, 4):
                row = scaled[(i - j - 1) * bs : (i - j) * bs]
                a_ref[b, part(i), (j + 1) * bs : (i + 1) * bs] -= dot_nt(
                    row, scaled[: (i - j) * bs]
                )
            a_ref[b, (j + 1) * bs :, part(j)] = scaled
            a_ref[b, part(j), part(j)] = invs[j][b]
    for b in range(nb):
        low_inv = invs[3][b]
        x2 = dot(a_ref[b, part(3), part(2)], a_ref[b, part(2), part(2)])
        x1 = dot(
            a_ref[b, part(3), part(1)] - dot(x2, a_ref[b, part(2), part(1)]),
            a_ref[b, part(1), part(1)],
        )
        x0 = dot(
            a_ref[b, part(3), part(0)]
            - dot(x1, a_ref[b, part(1), part(0)])
            - dot(x2, a_ref[b, part(2), part(0)]),
            a_ref[b, part(0), part(0)],
        )
        g_ref[b, :, part(3)] = low_inv
        for i, x in enumerate((x0, x1, x2)):
            g_ref[b, :, part(i)] = -dot(low_inv, x)
        at = [(row // blocks, row % blocks) for row in near_rows[b]] + [(me, first + b)]
        values = jnp.concatenate(
            [jnp.broadcast_to(values_ref[o, pl.ds(r, 1)], (chunk, bs)) for o, r in at], axis=1
        )
        w = dot_nt(values, g_ref[b])
        square = jnp.sum(w[:1] * w[:1], axis=1, keepdims=True)
        term = (logs[b] - 0.5 * square) * (1.0 / bs) - 0.5 * math.log(2.0 * math.pi)
        wt_ref[b] = jnp.concatenate([w, jnp.broadcast_to(term, w.shape)], axis=1)


def main_kernel(
    count, depth, capacity,
    near_ref, pos_ref, slot_ref, local_ref, points_ref, values_ref, probes_ref,
    rem_ref, tri_ref, w_ref, t_ref,
    a_ref, g_ref, wt_all, probes_all, q, z, sp,
    in1s, in1r, in2s, in2r, out1s, out1r, out2s, out2r, e1s, e1r, e2s, e2r,
    sb1, sb2, rb1, rb2, zsem, rsem, own_sem,
):
    me = lax.axis_index("rows")
    level = lax.axis_index("probe")
    blocks, cols, bs = probes_ref.shape
    total = blocks * count
    nb = g_ref.shape[0]
    cells = total * bs

    def position(b, j):
        ident = near_ref[me, b, j]
        return pos_ref[ident // blocks, 0, ident % blocks]

    def over_rows(i, source, target):
        return to_peers("rows", count, source, target, rsem.at[2 * i], rsem.at[2 * i + 1])

    def over_probe(i, source, target):
        return to_peers("probe", depth, source, target, zsem.at[2 * i], zsem.at[2 * i + 1])

    greet((("rows", count), ("probe", depth)))
    line = lax.broadcasted_iota(jnp.int32, (cols, bs), 0)
    here = pl.ds(me * blocks, blocks)
    probe_copies = over_rows(0, lambda peer: probes_ref, probes_all.at[here])
    keep = pltpu.make_async_copy(probes_ref, probes_all.at[here], own_sem)
    keep.start()

    first = level * nb
    near_rows = [[position(first + b, j) for j in range(3)] for b in range(nb)]
    build_kernels(near_rows, me, first, points_ref, a_ref)

    def inner(f):
        acc = jnp.zeros((cols, bs), jnp.float32)
        for c in range(total):
            acc = acc + f(c)
        return jnp.sum(acc, axis=1, keepdims=True)

    def send_in(i, source, s, r):
        for b in range(blocks):
            parts = [source[position(b, j)] for j in range(3)] + [source[me * blocks + b]]
            s[b // nb, b % nb] = jnp.concatenate(parts, axis=1)
        copies = over_probe(i, lambda peer: s.at[peer], r.at[level])
        r[level] = s[level]
        return copies

    keep.wait()
    wait_all(probe_copies)
    scale = 1.0 / jnp.sqrt(inner(lambda c: probes_all[c] * probes_all[c]) / cells + epsilon)
    for c in range(total):
        q[c] = probes_all[c] * scale
    in_copies = send_in(0, q, in1s, in1r)
    sp[3 * blocks] = jnp.zeros((cols, bs), jnp.float32)
    factor_blocks(near_rows, me, first, values_ref, a_ref, g_ref, wt_all.at[level])
    wt_copies = over_probe(1, lambda peer: wt_all.at[level], wt_all.at[level])

    def apply_operator(i, inr, outs, outr, es, er, sb, rb):
        energy = jnp.zeros((depth * cols, bs), jnp.float32)
        for b in range(nb):
            stacked = jnp.concatenate([inr[d, b] for d in range(depth)], axis=0)
            projected = dot_nt(stacked, g_ref[b])
            energy = energy + projected * projected
            spread = dot(projected, g_ref[b])
            for d in range(depth):
                outs[d, b] = spread[d * cols : (d + 1) * cols]
        for d in range(depth):
            es[d] = energy[d * cols : (d + 1) * cols]
        copies = over_probe(2 * i, lambda peer: outs.at[peer], outr.at[level])
        copies += over_probe(2 * i + 1, lambda peer: es.at[peer], er.at[level])
        outr[level] = outs[level]
        er[level] = es[level]
        wait_all(copies)
        energy = er[0]
        for d in range(1, depth):
            energy = energy + er[d]
        for b in range(blocks):
            for j in range(3):
                sp[b * 3 + j] = outr[b // nb, b % nb, :, j * bs : (j + 1) * bs]
        for d in range(count):
            for k in range(capacity):
                sb[d, k] = sp[slot_ref[d * capacity + k]]
            sb[d, capacity] = energy
            tile = jnp.full((cols, bs), -1, jnp.int32)
            for k in range(capacity):
                tile = jnp.where(line == k, local_ref[d * capacity + k], tile)
            sb[d, capacity + 1] = tile.astype(jnp.float32)
        copies = over_rows(i, lambda peer: sb.at[peer], rb.at[me])
        rb[me] = sb[me]
        wait_all(copies)
        sums = [outr[b // nb, b % nb, :, 3 * bs :] for b in range(blocks)]
        energy = jnp.zeros((cols, bs), jnp.float32)
        for d in range(count):
            tile = rb[d, capacity + 1]
            for k in range(capacity):
                value = rb[d, k]
                local = jnp.broadcast_to(tile[k : k + 1, :], (cols, bs))
                for b in range(blocks):
                    sums[b] = sums[b] + jnp.where(local == b, value, 0.0)
            energy = energy + rb[d, capacity]
        return sums, jnp.sum(energy, axis=1, keepdims=True) / cells

    wait_all(in_copies)
    image, alpha_one = apply_operator(1, in1r, out1s, out1r, e1s, e1r, sb1, rb1)
    for b in range(blocks):
        z[me * blocks + b] = image[b]
    wait_all(over_rows(2, lambda peer: z.at[here], z.at[here]))

    def residue(c):
        r = z[c] - alpha_one * q[c]
        return r * r

    beta_one = jnp.sqrt(inner(residue) / cells + epsilon)
    over = 1.0 / beta_one
    for b in range(blocks):
        rem_ref[b] = q[me * blocks + b]
    for c in range(total):
        q[c] = (z[c] - alpha_one * q[c]) * over
    wait_all(send_in(4, q, in2s, in2r))
    image, alpha_two = apply_operator(3, in2r, out2s, out2r, e2s, e2r, sb2, rb2)
    for b in range(blocks):
        rem_ref[b] = image[b] - alpha_two * q[me * blocks + b] - beta_one * rem_ref[b]
    lane = lax.broadcasted_iota(jnp.int32, (cols, bs), 1)
    tri_ref[...] = jnp.where(lane == 0, alpha_one, jnp.where(lane == 1, beta_one, alpha_two))
    wait_all(wt_copies)
    for b in range(blocks):
        w_ref[b : b + 1] = wt_all[b // nb, b % nb, :1, :bs]
        t_ref[b : b + 1] = wt_all[b // nb, b % nb, :1, bs:]


def main_call(count, depth, capacity, near, positions, slots, received, points, values, probes):
    blocks, cols, bs = probes.shape
    total = blocks * count
    nb = blocks // depth
    smem = pl.BlockSpec(memory_space=pltpu.SMEM)
    vmem = pl.BlockSpec(memory_space=pltpu.VMEM)
    f32 = jnp.float32
    dma = pltpu.SemaphoreType.DMA
    wide = pltpu.VMEM((depth, nb, cols, 4 * bs), f32)
    small = pltpu.VMEM((depth, cols, bs), f32)
    exchange = pltpu.VMEM((count, capacity + 2, cols, bs), f32)
    return pl.pallas_call(
        functools.partial(main_kernel, count, depth, capacity),
        out_shape=(
            jax.ShapeDtypeStruct((blocks, cols, bs), f32),
            jax.ShapeDtypeStruct((cols, bs), f32),
            jax.ShapeDtypeStruct((blocks, bs), f32),
            jax.ShapeDtypeStruct((blocks, bs), f32),
        ),
        in_specs=[smem] * 4 + [vmem] * 3,
        out_specs=(vmem,) * 4,
        scratch_shapes=[
            pltpu.VMEM((nb, 4 * bs, 4 * bs), f32),
            pltpu.VMEM((nb, bs, 4 * bs), f32),
            pltpu.VMEM((depth, nb, chunk, 2 * bs), f32),
            pltpu.VMEM((total, cols, bs), f32),
            pltpu.VMEM((total, cols, bs), f32),
            pltpu.VMEM((total, cols, bs), f32),
            pltpu.VMEM((3 * blocks + 1, cols, bs), f32),
        ]
        + [wide] * 8
        + [small] * 4
        + [exchange] * 4
        + [dma((16, depth - 1)), dma((8, count - 1)), dma],
        compiler_params=pltpu.CompilerParams(collective_id=1, has_side_effects=True),
    )(near, positions, slots, received, points, values, probes)


def body(points, observations, probes, neighbours, block_position):
    count = lax.axis_size("rows")
    depth = lax.axis_size("probe")
    blocks = points.shape[0]
    capacity = max(2, 6 * blocks // count)
    points_all, values_all, near_all, positions = gather_rows(
        count, (points, observations, neighbours, block_position.reshape(1, blocks))
    )
    first = lax.axis_index("rows").astype(jnp.int32).reshape(1)
    slots, received = plan_slots(first, near_all, positions, capacity)
    remainder, tri, whitened, terms = main_call(
        count, depth, capacity, near_all, positions, slots, received,
        points_all, values_all, probes,
    )
    return (whitened, terms[:, 0], tri[:, :3], remainder)


def solution(mesh):
    placed = (
        P("rows", None, None),
        P("rows", None),
        P("rows", "probe", None),
        P("rows", None),
        P("rows"),
    )
    return jax.shard_map(
        body,
        mesh=mesh,
        in_specs=placed,
        out_specs=(P("rows", None), P("rows"), P("probe", None), P("rows", "probe", None)),
        check_vma=False,
    )
```

```python
import functools
import math

import jax
import jax.numpy as jnp
from jax import lax
from jax.experimental import pallas as pl
from jax.experimental.pallas import tpu as pltpu
from jax.sharding import PartitionSpec as P

length_scale = 0.3
nugget = 0.25
epsilon = 1e-06
highest = lax.Precision.HIGHEST
chunk = 8


def dot(left, right):
    return jnp.dot(left, right, precision=highest, preferred_element_type=jnp.float32)


def dot_nt(left, right):
    return lax.dot_general(
        left, right, (((1,), (1,)), ((), ())), precision=highest,
        preferred_element_type=jnp.float32,
    )


def invert_pivots(cols, units):
    cols = list(cols)
    width = len(cols)
    low = list(units)
    diag = None

    def row(x, k):
        return jnp.broadcast_to(x[k : k + 1, :], x.shape)

    for k in range(0, width, 2):
        n = k + 1
        here, after = units[k] > 0.5, units[n] > 0.5
        a, b, c = row(cols[k], k), row(cols[n], k), row(cols[n], n)
        det = a * c - b * b
        over = 1.0 / det
        ratio = b * (1.0 / a)
        left, right = cols[k] - units[k], cols[n] - units[n]
        first = left * (c * over) - right * (b * over)
        second = right * (a * over) - left * (b * over)
        last = det * (1.0 / a)
        diag = a if diag is None else jnp.where(here, a, diag)
        diag = jnp.where(after, last, diag)
        for j in range(width):
            if j != k and j != n:
                upper, lower = row(cols[j], k), row(cols[j], n)
                if j < k:
                    low[j] = jnp.where(here, upper, low[j])
                    low[j] = jnp.where(after, lower - ratio * upper, low[j])
                cols[j] = cols[j] - (first * upper + second * lower)
        low[k] = jnp.where(after, -ratio, low[k])
        cols[k] = units[k] - first
        cols[n] = units[n] - second
        yield cols, low, diag


def weighted(parts, rows):
    terms = [p * r for p, r in zip(parts, rows)]
    while len(terms) > 1:
        terms = [a + b for a, b in zip(terms[::2], terms[1::2])] + terms[len(terms) & ~1 :]
    return terms[0]


def sweep(mats):
    pairs = [(mats[i], mats[min(i + 1, len(mats) - 1)]) for i in range(0, len(mats), 2)]
    count = len(mats[0])
    shape = mats[0][0].shape
    half = shape[1] // 2
    lane = lax.broadcasted_iota(jnp.int32, shape, 1)
    sub = lax.broadcasted_iota(jnp.int32, shape, 0)
    left = lane < half
    place = jnp.where(left, lane, lane - half)
    units = [jnp.where(sub == k, 1.0, 0.0) for k in range(chunk)]

    def full(x):
        return jnp.broadcast_to(x, shape)

    def swap(x):
        return pltpu.roll(x, half, 1)

    def pick(x, at):
        return jnp.where(left, full(x[:, at : at + 1]), full(x[:, half + at : half + at + 1]))

    packed = [
        [
            [jnp.where(left, x, swap(y)) for x, y in zip(one, two)],
            [jnp.where(left, swap(x), y) for x, y in zip(one, two)],
        ]
        for one, two in pairs
    ]
    logs = [jnp.zeros(shape, jnp.float32) for _ in pairs]
    waiting = []
    for t in range(count):
        side, o = divmod(t * chunk, half)
        picked = (place >= o) & (place < o + chunk)
        unit = jnp.where(place == sub + o, 1.0, 0.0)
        steps = [
            invert_pivots([pick(sides[side][t], o + k) for k in range(chunk)], units)
            for sides in packed
        ]
        found = None
        for k in range(0, chunk, 2):
            found = [next(step) for step in steps]
            share = -(-len(waiting) * 2 // (chunk - k))
            for update in waiting[:share]:
                update()
            waiting = waiting[share:]
        later = []
        for n, (sides, (inv, low, diag)) in enumerate(zip(packed, found)):
            scale = lax.rsqrt(diag)
            logs[n] = logs[n] + jnp.log(diag)
            r = []
            for s in range(2):
                rows = jnp.where(picked, unit, sides[s][t]) if s == side else sides[s][t]
                rows = [full(rows[k : k + 1, :]) for k in range(chunk)]
                move = weighted(inv, rows)
                sides[s][t] = scale * weighted(low, rows)
                r.append([full(move[k : k + 1, :]) for k in range(chunk)])

            def update(p, sides=sides, r=r, side=side, o=o, picked=picked):
                cols = [pick(sides[side][p], o + k) for k in range(chunk)]
                for s in range(2):
                    old = jnp.where(picked, 0.0, sides[s][p]) if s == side else sides[s][p]
                    sides[s][p] = old - weighted(cols, r[s])

            if t + 1 < count:
                update(t + 1)
            later.append([functools.partial(update, p) for p in range(t + 2, count)])
        waiting = [u for group in zip(*later) for u in group]
    out, sums = [], []
    for sides, total in zip(packed, logs):
        out.append([jnp.where(left, x, swap(y)) for x, y in zip(*sides)])
        out.append([jnp.where(left, swap(x), y) for x, y in zip(*sides)])
        total = -0.5 * jnp.sum(total, axis=0, keepdims=True)
        sums += [total[:, :1], total[:, half : half + 1]]
    return out[: len(mats)], sums[: len(mats)]


MESH = pl.DeviceIdType.MESH


def to_peers(axis, count, source, target, send_sem, recv_sem):
    me = lax.axis_index(axis)
    copies = []
    for p in range(1, count):
        peer = lax.rem(me + p, count)
        copies.append(
            pltpu.make_async_remote_copy(
                src_ref=source(peer),
                dst_ref=target,
                send_sem=send_sem.at[p - 1],
                recv_sem=recv_sem.at[p - 1],
                device_id={axis: peer},
                device_id_type=MESH,
            )
        )
    for copy in copies:
        copy.start()
    return copies


def wait_all(copies):
    for copy in copies:
        copy.wait()


def greet(counts):
    barrier = pltpu.get_barrier_semaphore()
    total = 0
    for axis, count in counts:
        for p in range(1, count):
            peer = lax.rem(lax.axis_index(axis) + p, count)
            pl.semaphore_signal(barrier, inc=1, device_id={axis: peer}, device_id_type=MESH)
            total += 1
    pl.semaphore_wait(barrier, total)


def gather_kernel(count, *refs):
    half = 4
    sources, targets, (send_sem, recv_sem, own_sem) = refs[:half], refs[half : 2 * half], refs[2 * half :]
    me = lax.axis_index("rows")
    greet((("rows", count),))
    copies = []
    for i in range(half):
        copies += to_peers(
            "rows", count, lambda peer: sources[i], targets[i].at[me], send_sem.at[i], recv_sem.at[i]
        )
    owns = [
        pltpu.make_async_copy(sources[i], targets[i].at[me], own_sem.at[i]) for i in range(half)
    ]
    for own in owns:
        own.start()
    for own in owns:
        own.wait()
    wait_all(copies)


def gather_rows(count, arrays):
    vmem = pl.BlockSpec(memory_space=pltpu.VMEM)
    return pl.pallas_call(
        functools.partial(gather_kernel, count),
        out_shape=[jax.ShapeDtypeStruct((count,) + a.shape, a.dtype) for a in arrays],
        in_specs=[vmem] * len(arrays),
        out_specs=[vmem] * len(arrays),
        scratch_shapes=[
            pltpu.SemaphoreType.DMA((len(arrays), count - 1)),
            pltpu.SemaphoreType.DMA((len(arrays), count - 1)),
            pltpu.SemaphoreType.DMA((len(arrays),)),
        ],
        compiler_params=pltpu.CompilerParams(collective_id=0, has_side_effects=True),
    )(*arrays)


def plan_kernel(capacity, depth, first_ref, near_ref, pos_ref, slot_ref, local_ref, seen_ref):
    count, blocks = near_ref.shape[0], near_ref.shape[2]
    me = first_ref[0]

    def position(owner, b, j):
        ident = near_ref[owner, j, b]
        return pos_ref[ident // blocks, 0, ident % blocks]

    nb = blocks // depth
    tiles = 4 * nb + 1
    for i in range(count * capacity):
        slot_ref[i] = depth * tiles
        local_ref[i] = -1
    for i in range(count):
        seen_ref[i] = 0

    def place_own(b, c):
        for j in range(3):
            row = position(me, b, j)
            at = row // blocks
            rank = seen_ref[at]
            seen_ref[at] = rank + 1
            slot_ref[at * capacity + rank] = b // nb * tiles + b % nb * 4 + j
            local_ref[at * capacity + rank] = row % blocks
        return c

    lax.fori_loop(0, blocks, place_own, 0)


def plan_slots(first, near, positions, capacity, depth):
    count = near.shape[0]
    smem = pl.BlockSpec(memory_space=pltpu.SMEM)
    slots = jax.ShapeDtypeStruct((count * capacity,), jnp.int32)
    return pl.pallas_call(
        functools.partial(plan_kernel, capacity, depth),
        out_shape=(slots, slots),
        in_specs=[smem] * 3,
        out_specs=(smem, smem),
        scratch_shapes=[pltpu.SMEM((count,), jnp.int32)],
    )(first, near, positions)


def build_kernels(near_rows, me, first, points_ref, a_ref):
    nb = a_ref.shape[0]
    _, blocks, bs = points_ref.shape[1:]

    def part(i):
        return slice(i * bs, (i + 1) * bs)

    same = lax.broadcasted_iota(jnp.int32, (bs, bs), 0) == lax.broadcasted_iota(
        jnp.int32, (bs, bs), 1
    )
    for b in range(nb):
        at = [(row // blocks, row % blocks) for row in near_rows[b]] + [(me, first + b)]
        rows = [[points_ref[o, c, pl.ds(r, 1), :] for c in range(3)] for o, r in at]
        pad = jnp.zeros((chunk - 3, bs), jnp.float32)
        cols = [jnp.transpose(jnp.concatenate(row + [pad], axis=0)) for row in rows]
        for i in range(4):
            for k in range(i + 1):
                dist_sq = None
                for c in range(3):
                    off = cols[i][:, c : c + 1] - rows[k][c]
                    dist_sq = off * off if dist_sq is None else dist_sq + off * off
                value = 1.0 / (1.0 + dist_sq * (1.0 / (length_scale * length_scale)))
                if i == k:
                    value = value + jnp.where(same, nugget, 0.0)
                a_ref[b, part(i), part(k)] = value


def factor_blocks(near_rows, me, first, values_ref, a_ref, g_ref, wt_ref, midway):
    nb, bs = g_ref.shape[:2]
    blocks = values_ref.shape[1]

    def part(i):
        return slice(i * bs, (i + 1) * bs)

    def load(j):
        return tuple(
            tuple(
                a_ref[b, j * bs + i * chunk : j * bs + (i + 1) * chunk, part(j)]
                for i in range(bs // chunk)
            )
            for b in range(nb)
        )

    below = lax.broadcasted_iota(jnp.int32, (bs, bs), 0) >= lax.broadcasted_iota(
        jnp.int32, (bs, bs), 1
    )
    invs = []
    for j in range(4):
        low, logs = sweep(load(j))
        invs.append([jnp.where(below, jnp.concatenate(low[b], axis=0), 0.0) for b in range(nb)])
        if j == 3:
            break
        if j == 0:
            midway()
        for b in range(nb):
            scaled = dot_nt(a_ref[b, (j + 1) * bs :, part(j)], invs[j][b])
            for i in range(j + 1, 4):
                row = scaled[(i - j - 1) * bs : (i - j) * bs]
                a_ref[b, part(i), (j + 1) * bs : (i + 1) * bs] -= dot_nt(
                    row, scaled[: (i - j) * bs]
                )
            a_ref[b, (j + 1) * bs :, part(j)] = scaled
            a_ref[b, part(j), part(j)] = invs[j][b]
    for b in range(nb):
        low_inv = invs[3][b]
        x2 = dot(a_ref[b, part(3), part(2)], a_ref[b, part(2), part(2)])
        x1 = dot(
            a_ref[b, part(3), part(1)] - dot(x2, a_ref[b, part(2), part(1)]),
            a_ref[b, part(1), part(1)],
        )
        x0 = dot(
            a_ref[b, part(3), part(0)]
            - dot(x1, a_ref[b, part(1), part(0)])
            - dot(x2, a_ref[b, part(2), part(0)]),
            a_ref[b, part(0), part(0)],
        )
        g_ref[b, :, part(3)] = low_inv
        for i, x in enumerate((x0, x1, x2)):
            g_ref[b, :, part(i)] = -dot(low_inv, x)
        at = [(row // blocks, row % blocks) for row in near_rows[b]] + [(me, first + b)]
        values = jnp.concatenate(
            [jnp.broadcast_to(values_ref[o, pl.ds(r, 1)], (chunk, bs)) for o, r in at], axis=1
        )
        w = dot_nt(values, g_ref[b])
        square = jnp.sum(w[:1] * w[:1], axis=1, keepdims=True)
        term = (logs[b] - 0.5 * square) * (1.0 / bs) - 0.5 * math.log(2.0 * math.pi)
        wt_ref[b] = jnp.concatenate([w, jnp.broadcast_to(term, w.shape)], axis=1)


def main_kernel(
    count, depth, capacity,
    near_ref, pos_ref, slot_ref, local_ref, points_ref, values_ref, probes_ref,
    rem_ref, tri_ref, w_ref, t_ref,
    a_ref, g_ref, wt_all, probes_all, q, q2, z, lts, ltr,
    ins, inr, outs, outr, sbs, rbs, zsem, rsem, own_sem,
):
    me = lax.axis_index("rows")
    level = lax.axis_index("probe")
    blocks, cols, bs = probes_ref.shape
    parts = len(z)
    span = cols // parts
    total = blocks * count
    nb = g_ref.shape[0]
    cells = total * bs

    def position(b, j):
        ident = near_ref[me, j, b]
        return pos_ref[ident // blocks, 0, ident % blocks]

    def over_rows(i, source, target):
        return to_peers("rows", count, source, target, rsem.at[2 * i], rsem.at[2 * i + 1])

    def over_probe(i, source, target):
        return to_peers("probe", depth, source, target, zsem.at[2 * i], zsem.at[2 * i + 1])

    greet((("rows", count), ("probe", depth)))
    here = pl.ds(me * blocks, blocks)
    probe_copies = over_rows(0, lambda peer: probes_ref, probes_all.at[here])
    keep = pltpu.make_async_copy(probes_ref, probes_all.at[here], own_sem)
    keep.start()

    first = level * nb
    near_rows = [[position(first + b, j) for j in range(3)] for b in range(nb)]
    build_kernels(near_rows, me, first, points_ref, a_ref)

    def inner(f):
        acc = [jnp.zeros((span, bs), jnp.float32) for _ in range(4)]
        for c in range(total):
            acc[c % 4] = acc[c % 4] + f(c)
        acc = (acc[0] + acc[1]) + (acc[2] + acc[3])
        return jnp.sum(acc, axis=1, keepdims=True)

    def rows_of(h):
        return slice(h * span, (h + 1) * span)

    def send_in(i, h, source):
        s, r = ins[i][h], inr[i][h]
        for b in range(blocks):
            at = [position(b, j) for j in range(3)] + [me * blocks + b]
            for j in range(4):
                s[b // nb, b % nb * 4 + j] = source[at[j]]
        copies = over_probe(1 + i * parts + h, lambda peer: s.at[peer], r.at[level])
        r[level] = s[level]
        return copies

    early = []

    def midway():
        keep.wait()
        wait_all(probe_copies)
        for h in range(parts):
            def part_of(c):
                return probes_all[c, rows_of(h), :]

            scale = 1.0 / jnp.sqrt(inner(lambda c: part_of(c) * part_of(c)) / cells + epsilon)
            for c in range(total):
                q[h][c] = part_of(c) * scale
            early.append(send_in(0, h, q[h]))
        line = lax.broadcasted_iota(jnp.int32, lts.shape[1:], 0)
        for d in range(count):
            tile = jnp.full(lts.shape[1:], -1, jnp.int32)
            for k in range(capacity):
                tile = jnp.where(line == k, local_ref[d * capacity + k], tile)
            lts[d] = tile.astype(jnp.float32)
        early.append(over_rows(1, lambda peer: lts.at[peer], ltr.at[me]))
        ltr[me] = lts[me]
        for i in range(2):
            for h in range(parts):
                outr[i][h][depth * (4 * nb + 1)] = jnp.zeros((span, bs), jnp.float32)

    factor_blocks(near_rows, me, first, values_ref, a_ref, g_ref, wt_all.at[level], midway)
    wt_copies = over_probe(0, lambda peer: wt_all.at[level], wt_all.at[level])
    tiles = 4 * nb + 1

    def multiply(i, h):
        source, s, r = inr[i][h], outs[i][h], outr[i][h]
        energy = jnp.zeros((depth * span, bs), jnp.float32)
        for b in range(nb):
            stacked = jnp.concatenate(
                [
                    jnp.concatenate([source[d, b * 4 + j] for j in range(4)], axis=1)
                    for d in range(depth)
                ],
                axis=0,
            )
            projected = dot_nt(stacked, g_ref[b])
            energy = energy + projected * projected
            spread = dot(projected, g_ref[b])
            for d in range(depth):
                for j in range(4):
                    s[d, b * 4 + j] = spread[d * span : (d + 1) * span, j * bs : (j + 1) * bs]
        for d in range(depth):
            s[d, 4 * nb] = energy[d * span : (d + 1) * span]
        copies = over_probe(
            1 + (2 + i) * parts + h, lambda peer: s.at[peer], r.at[pl.ds(level * tiles, tiles)]
        )
        r[pl.ds(level * tiles, tiles)] = s[level]
        return copies

    def transpose_out(i, h):
        source, s, r = outr[i][h], sbs[i][h], rbs[i][h]
        energy = source[4 * nb]
        for d in range(1, depth):
            energy = energy + source[d * tiles + 4 * nb]
        for d in range(count):
            for k in range(capacity):
                s[d, k] = source[slot_ref[d * capacity + k]]
            s[d, capacity] = energy
        copies = over_rows(2 + i * parts + h, lambda peer: s.at[peer], r.at[me])
        r[me] = s[me]
        return copies

    def collect(i, h):
        source, r = outr[i][h], rbs[i][h]
        sums = [source[b // nb * tiles + b % nb * 4 + 3] for b in range(blocks)]
        energy = jnp.zeros((span, bs), jnp.float32)
        for d in range(count):
            tile = ltr[d]
            for k in range(capacity):
                value = r[d, k]
                local = jnp.broadcast_to(tile[k : k + 1, :], (span, bs))
                for b in range(blocks):
                    sums[b] = sums[b] + jnp.where(local == b, value, 0.0)
            energy = energy + r[d, capacity]
        return sums, jnp.sum(energy, axis=1, keepdims=True) / cells

    def share(h):
        image, alpha = collect(0, h)
        for b in range(blocks):
            z[h][me * blocks + b] = image[b]
        return alpha, over_rows(2 + 2 * parts + h, lambda peer: z[h].at[here], z[h].at[here])

    def second(h, alpha):
        def residue(c):
            r = z[h][c] - alpha * q[h][c]
            return r * r

        beta = jnp.sqrt(inner(residue) / cells + epsilon)
        over = 1.0 / beta
        for c in range(total):
            q2[h][c] = (z[h][c] - alpha * q[h][c]) * over
        return beta, send_in(1, h, q2[h])

    every = range(parts)
    flying = []
    for h in every:
        wait_all(early[h])
        flying.append(multiply(0, h))
    for h in every:
        wait_all(flying[h])
        flying[h] = transpose_out(0, h)
    wait_all(early[parts])
    alpha_one, beta_one, alpha_two = {}, {}, {}
    for h in every:
        wait_all(flying[h])
        alpha_one[h], flying[h] = share(h)
    for h in every:
        wait_all(flying[h])
        beta_one[h], flying[h] = second(h, alpha_one[h])
    for h in every:
        wait_all(flying[h])
        flying[h] = multiply(1, h)
    for h in every:
        wait_all(flying[h])
        flying[h] = transpose_out(1, h)
    wait_all(wt_copies)
    for b in range(blocks):
        w_ref[b : b + 1] = wt_all[b // nb, b % nb, :1, :bs]
    terms = jnp.concatenate([wt_all[b // nb, b % nb, :1, bs:] for b in range(blocks)], axis=0)
    t_ref[...] = jnp.transpose(terms)[:1, :]
    for h in every:
        wait_all(flying[h])
        image, alpha_two[h] = collect(1, h)
        for b in range(blocks):
            rem_ref[b, rows_of(h), :] = (
                image[b] - alpha_two[h] * q2[h][me * blocks + b]
                - beta_one[h] * q[h][me * blocks + b]
            )
    lane = lax.broadcasted_iota(jnp.int32, (cols, bs), 1)

    def joined(x):
        return jnp.concatenate([x[h] for h in every], axis=0)

    tri = jnp.where(
        lane == 0, joined(alpha_one), jnp.where(lane == 1, joined(beta_one), joined(alpha_two))
    )
    tri_ref[...] = jnp.transpose(tri)[:3, :]


def main_call(count, depth, capacity, near, positions, slots, received, points, values, probes):
    blocks, cols, bs = probes.shape
    total = blocks * count
    nb = blocks // depth
    parts = max(1, cols // chunk)
    span = cols // parts
    smem = pl.BlockSpec(memory_space=pltpu.SMEM)
    vmem = pl.BlockSpec(memory_space=pltpu.VMEM)
    f32 = jnp.float32
    dma = pltpu.SemaphoreType.DMA

    def each(*shape):
        return [pltpu.VMEM(shape, f32) for _ in range(parts)]

    def both(*shape):
        return [each(*shape), each(*shape)]

    return pl.pallas_call(
        functools.partial(main_kernel, count, depth, capacity),
        out_shape=(
            jax.ShapeDtypeStruct((blocks, cols, bs), f32),
            jax.ShapeDtypeStruct((3, cols), f32),
            jax.ShapeDtypeStruct((blocks, bs), f32),
            jax.ShapeDtypeStruct((1, blocks), f32),
        ),
        in_specs=[smem] * 4 + [vmem] * 3,
        out_specs=(vmem,) * 4,
        scratch_shapes=[
            pltpu.VMEM((nb, 4 * bs, 4 * bs), f32),
            pltpu.VMEM((nb, bs, 4 * bs), f32),
            pltpu.VMEM((depth, nb, chunk, 2 * bs), f32),
            pltpu.VMEM((total, cols, bs), f32),
            each(total, span, bs),
            each(total, span, bs),
            each(total, span, bs),
            pltpu.VMEM((count, chunk, bs), f32),
            pltpu.VMEM((count, chunk, bs), f32),
            both(depth, nb * 4, span, bs),
            both(depth, nb * 4, span, bs),
            both(depth, nb * 4 + 1, span, bs),
            both(depth * (nb * 4 + 1) + 1, span, bs),
            both(count, capacity + 1, span, bs),
            both(count, capacity + 1, span, bs),
            dma((2 * (4 * parts + 1), depth - 1)),
            dma((2 * (3 * parts + 2), count - 1)),
            dma,
        ],
        compiler_params=pltpu.CompilerParams(collective_id=1, has_side_effects=True),
    )(near, positions, slots, received, points, values, probes)


def hand_kernel(*refs):
    half = len(refs) // 2
    for source, target in zip(refs[:half], refs[half:]):
        target[...] = source[...]


def hand_over(arrays):
    vmem = pl.BlockSpec(memory_space=pltpu.VMEM)
    return pl.pallas_call(
        hand_kernel,
        out_shape=[jax.ShapeDtypeStruct(a.shape, a.dtype) for a in arrays],
        in_specs=[vmem] * len(arrays),
        out_specs=[vmem] * len(arrays),
    )(*arrays)


def body(points, observations, probes, neighbours, block_position):
    count = lax.axis_size("rows")
    depth = lax.axis_size("probe")
    blocks = points.shape[0]
    capacity = max(2, 6 * blocks // count)
    points_all, values_all, near_all, positions = gather_rows(
        count,
        (
            jnp.transpose(points, (1, 0, 2)), observations, neighbours.T,
            block_position.reshape(1, blocks),
        ),
    )
    first = lax.axis_index("rows").astype(jnp.int32).reshape(1)
    slots, received = plan_slots(first, near_all, positions, capacity, depth)
    remainder, tri, whitened, terms = main_call(
        count, depth, capacity, near_all, positions, slots, received,
        points_all, values_all, probes,
    )
    remainder, tri, whitened, terms = hand_over((remainder, tri, whitened, terms))
    return (whitened, terms.reshape(blocks), tri.T, remainder)


def solution(mesh):
    placed = (
        P("rows", None, None),
        P("rows", None),
        P("rows", "probe", None),
        P("rows", None),
        P("rows"),
    )
    return jax.shard_map(
        body,
        mesh=mesh,
        in_specs=placed,
        out_specs=(P("rows", None), P("rows"), P("probe", None), P("rows", "probe", None)),
        check_vma=False,
    )
```
